256 devices in a mesh: node: 4 (over x), replica: 64 (over z, y, core).
Axes of the slice: x: 4, y: 4, z: 8, core: 2. Of those that a mesh axis runs over, the one named last changes fastest.
Arguments:
- inputs: bfloat16 [131072, 1024], P(('node', 'replica')), may hold values from -8 to 8
- grads_out: bfloat16 [131072, 1024], P(('node', 'replica')), may hold values from -1 to 1
- lengths: int32 [1024], P(('node', 'replica')), may hold values from 32 to 128
- w_in: bfloat16 [1024, 2048], P(None, 'node'), may hold values from -0.5 to 0.5
- bias_in: bfloat16 [2048], P('node'), may hold values from -3 to 3
- w_out: bfloat16 [2048, 1024], P('node'), may hold values from -0.4 to 0.4
Outputs:
- grad_w_in: float32 [1024, 2048], P('replica', 'node')
- grad_w_out: float32 [2048, 1024], P(('node', 'replica'))
- grad_bias_in: float32 [2048], P(('node', 'replica'))
- grad_bias_out: float32 [1024], P(('node', 'replica'))
The draws below stay inside these ranges and needn't reach their ends.
All inputs are finite; a program needn't handle non-finite values.
Results may differ from the reference program's by a relative error of at most 0.0003.
Values may be sent and summed in bfloat16 or wider, within the bound.
A program may use at most 64 MiB of HBM per device.

```python
import math
import jax
import jax.numpy as jnp
from jax import lax

D = 1024
FF = 2048
SEQ = 128
TOK_DEV = 512
TOKENS = 131072
SEQS = 1024
N_NODE = 4
N_REPLICA = 64


def draw_inputs(key, part):
    key_mean, key_noise = jax.random.split(jax.random.fold_in(key, 11), 2)
    mean_row = jnp.clip(jax.random.normal(key_mean, (1, D), jnp.float32), -4.0, 4.0)
    noise = jnp.clip(jax.random.normal(key_noise, (TOKENS, D), jnp.float32), -4.0, 4.0)
    values = 0.8 * mean_row + noise
    return jnp.clip(values, -8.0, 8.0).astype(jnp.bfloat16)


def draw_grads_out(key, part):
    key_mean, key_noise, key_rows = jax.random.split(jax.random.fold_in(key, 23), 3)
    mean_row = jnp.clip(jax.random.normal(key_mean, (1, D), jnp.float32), -4.0, 4.0)
    row_index = jnp.arange(TOKENS, dtype=jnp.int32) % (TOKENS // N_NODE)
    ramp = jnp.exp(math.log(10.0) * row_index.astype(jnp.float32) / (TOKENS // N_NODE)).reshape(TOKENS, 1)
    row_scale = jnp.exp(jax.random.uniform(key_rows, (TOKENS, 1), jnp.float32, 0.0, math.log(3.0)))
    column_pos = jnp.arange(D, dtype=jnp.int32).astype(jnp.float32).reshape(1, D) / D
    noise = jnp.clip(jax.random.normal(key_noise, (TOKENS, D), jnp.float32), -4.0, 4.0)
    values = mean_row + noise
    column_scale = jnp.exp(math.log(3.0) * column_pos)
    values = ramp * row_scale * column_scale * values / (4.0 * TOK_DEV)
    return jnp.clip(values, -1.0, 1.0).astype(jnp.bfloat16)


def draw_w_in(key, part):
    key_noise = jax.random.fold_in(key, 37)
    column_pos = jnp.arange(FF, dtype=jnp.int32).astype(jnp.float32).reshape(1, FF) / FF
    noise = jnp.clip(jax.random.normal(key_noise, (D, FF), jnp.float32), -6.0, 6.0)
    column_scale = 0.5 * jnp.exp(math.log(4.0) * column_pos)
    values = noise * column_scale / math.sqrt(D)
    return jnp.clip(values, -0.5, 0.5).astype(jnp.bfloat16)


def draw_w_out(key, part):
    key_noise = jax.random.fold_in(key, 41)
    row_pos = jnp.arange(FF, dtype=jnp.int32).astype(jnp.float32).reshape(FF, 1) / FF
    noise = jnp.clip(jax.random.normal(key_noise, (FF, D), jnp.float32), -6.0, 6.0)
    row_scale = 0.4 * jnp.exp(math.log(5.0) * row_pos)
    values = noise * row_scale / math.sqrt(FF)
    return jnp.clip(values, -0.4, 0.4).astype(jnp.bfloat16)


def plant(values, key, smallest, high):
    index_at = [jax.random.randint(jax.random.fold_in(key, axis), (), 0, length) for axis, length in enumerate(values.shape)]
    main_axis = values.shape.index(max(values.shape))
    neighbour = index_at[:main_axis] + [(index_at[main_axis] + 1) % values.shape[main_axis]] + index_at[main_axis + 1:]
    return values.at[tuple(index_at)].set(smallest).at[tuple(neighbour)].set(high)


def shard_levels(stream_key, shape, cuts, low, largest):
    def one(dim, shards_of):
        steps = jax.random.uniform(jax.random.fold_in(jax.random.fold_in(stream_key, 6), dim), (shards_of,), jnp.float32, low / len(cuts), largest / len(cuts))
        return jnp.repeat(jnp.exp(steps), shape[dim] // shards_of).reshape((-1,) + (1,) * (len(shape) - dim - 1))

    factor_of = one(*cuts[0])
    for cut in cuts[1:]:
        factor_of = factor_of * one(*cut)
    return factor_of


def centred(own_key, dims, scale, limit, cuts=(), kind=jnp.bfloat16):
    loudness = shard_levels(own_key, dims, cuts, -0.22, 0.18) if cuts else 1.0
    values = jax.random.normal(own_key, dims, jnp.float32) * scale * loudness
    return jnp.minimum(jnp.maximum(values, -limit), limit).astype(kind)


def setup_inputs(seed: int = 0) -> dict:
    seeds = jax.random.split(jax.random.key(seed), 7)
    inputs = draw_inputs(jax.random.fold_in(seeds[6], 71), 0)
    grads_out = draw_grads_out(jax.random.fold_in(seeds[6], 71), 0)
    lengths = plant(jax.random.randint(seeds[2], (SEQS,), SEQ // 4, SEQ + 1), jax.random.fold_in(seeds[2], 1), SEQ // 4, SEQ).astype(jnp.int32)
    w_in = draw_w_in(jax.random.fold_in(seeds[6], 71), 0)
    bias_in = centred(seeds[4], (FF,), 0.5, 3.0, ((0, 4),))
    w_out = draw_w_out(jax.random.fold_in(seeds[6], 71), 0)
    return dict(inputs=inputs, grads_out=grads_out, lengths=lengths, w_in=w_in, bias_in=bias_in, w_out=w_out)


root_half = 0.7071067811865476
inv_root_tau = 0.3989422804014327
eps_norm = 1e-6


def masked_cotangent(grads_out, lengths):
    row_count = grads_out.shape[0]
    position = lax.broadcasted_iota(jnp.int32, (row_count // SEQ, SEQ), 1)
    keep_mask = (position < lengths[:, None]).reshape(row_count, 1)
    return jnp.where(keep_mask, grads_out, jnp.zeros_like(grads_out))


def layer_grads(inputs, cotangent, w_in, bias_in, w_out):
    preact = jnp.dot(inputs, w_in, preferred_element_type=jnp.float32) + bias_in.astype(jnp.float32)
    normal_cdf = 0.5 * (1.0 + jax.scipy.special.erf(preact * root_half))
    activated = (preact * normal_cdf).astype(jnp.bfloat16)
    grad_act = lax.dot_general(cotangent, w_out, (((1,), (1,)), ((), ())), preferred_element_type=jnp.float32)
    grad_pre = grad_act * (normal_cdf + preact * inv_root_tau * jnp.exp(-0.5 * preact * preact))
    grad_half = grad_pre.astype(jnp.bfloat16)
    grad_in = lax.dot_general(inputs, grad_half, (((0,), (0,)), ((), ())), preferred_element_type=jnp.float32)
    grad_out = lax.dot_general(activated, cotangent, (((0,), (0,)), ((), ())), preferred_element_type=jnp.float32)
    return (grad_in, grad_out, jnp.sum(grad_pre, 0), jnp.sum(cotangent.astype(jnp.float32), 0))


def weigh_pair(first_parts, second_parts, totals):
    merged = []
    for index_now in range(len(first_parts)):
        cross = totals[index_now][0]
        first_sq = totals[index_now][1]
        second_sq = totals[index_now][2]
        first_coef = 1.0 - cross / (2.0 * (first_sq + eps_norm))
        second_coef = 1.0 - cross / (2.0 * (second_sq + eps_norm))
        merged.append(first_coef * first_parts[index_now] + second_coef * second_parts[index_now])
    return tuple(merged)


def adasum_pair(first_parts, second_parts):
    totals = []
    for first_part, second_part in zip(first_parts, second_parts):
        totals.append((jnp.sum(first_part * second_part), jnp.sum(first_part * first_part), jnp.sum(second_part * second_part)))
    return weigh_pair(first_parts, second_parts, totals)


def reference(inputs, grads_out, lengths, w_in, bias_in, w_out):
    cotangent = masked_cotangent(grads_out, lengths)
    depth_count = N_REPLICA.bit_length() - 1
    shaped_inputs = inputs.reshape(N_NODE, N_REPLICA, TOK_DEV, D)
    shaped_cotangent = cotangent.reshape(N_NODE, N_REPLICA, TOK_DEV, D)

    def leaf_grads(leaf_order):
        replica = jnp.zeros((), jnp.int32)
        for depth_now in range(depth_count):
            replica = replica + ((leaf_order >> depth_now) & 1) * (1 << (depth_count - 1 - depth_now))
        rows_in = lax.dynamic_index_in_dim(shaped_inputs, replica, 1, keepdims=False).reshape(N_NODE * TOK_DEV, D)
        rows_cot = lax.dynamic_index_in_dim(shaped_cotangent, replica, 1, keepdims=False).reshape(N_NODE * TOK_DEV, D)
        return layer_grads(rows_in, rows_cot, w_in, bias_in, w_out)

    shapes = [(D, FF), (FF, D), (FF,), (D,)]
    stack_init = tuple(jnp.zeros((max(depth_count, 1),) + shape_now, jnp.float32) for shape_now in shapes)
    item_init = tuple(jnp.zeros(shape_now, jnp.float32) for shape_now in shapes)

    def step_leaf(state_now, leaf_order):
        stacks = state_now[0]
        current = leaf_grads(leaf_order)
        finished = jnp.zeros((), jnp.bool_)
        for depth_now in range(depth_count):
            occupied = ((leaf_order >> depth_now) & 1) == 1
            stored = tuple(stack_now[depth_now] for stack_now in stacks)
            merged = adasum_pair(stored, current)
            place = jnp.logical_and(jnp.logical_not(finished), jnp.logical_not(occupied))
            absorb = jnp.logical_and(jnp.logical_not(finished), occupied)
            stacks = tuple(stack_now.at[depth_now].set(jnp.where(place, part_now, stack_now[depth_now])) for stack_now, part_now in zip(stacks, current))
            current = tuple(jnp.where(absorb, merged_part, part_now) for merged_part, part_now in zip(merged, current))
            finished = jnp.logical_or(finished, place)
        return (stacks, current), None

    final_state, unused = lax.scan(step_leaf, (stack_init, item_init), jnp.arange(N_REPLICA, dtype=jnp.int32))
    result = final_state[1]
    return (result[0], result[1], result[2], result[3])
```

```python
import jax
import jax.numpy as jnp
from jax import lax
from jax.experimental import pallas as pl
from jax.experimental.pallas import tpu as pltpu
from jax.sharding import PartitionSpec as P

SEQ = 128


root_half = 0.7071067811865476
inv_root_tau = 0.3989422804014327
eps_norm = 1e-06


def masked_cotangent(grads_out, lengths):
    row_count = grads_out.shape[0]
    position = lax.broadcasted_iota(jnp.int32, (row_count // SEQ, SEQ), 1)
    keep_mask = (position < lengths[:, None]).reshape(row_count, 1)
    return jnp.where(keep_mask, grads_out, jnp.zeros_like(grads_out))


def layer_grads(inputs, cotangent, w_in, bias_in, w_out):
    preact = jnp.dot(inputs, w_in, preferred_element_type=jnp.float32) + bias_in.astype(jnp.float32)
    normal_cdf = 0.5 * (1.0 + jax.scipy.special.erf(preact * root_half))
    activated = (preact * normal_cdf).astype(jnp.bfloat16)
    grad_act = lax.dot_general(
        cotangent, w_out, (((1,), (1,)), ((), ())), preferred_element_type=jnp.float32
    )
    grad_pre = grad_act * (normal_cdf + preact * inv_root_tau * jnp.exp(-0.5 * preact * preact))
    grad_half = grad_pre.astype(jnp.bfloat16)
    grad_in = lax.dot_general(
        inputs, grad_half, (((0,), (0,)), ((), ())), preferred_element_type=jnp.float32
    )
    grad_out = lax.dot_general(
        activated, cotangent, (((0,), (0,)), ((), ())), preferred_element_type=jnp.float32
    )
    return (grad_in, grad_out, jnp.sum(grad_pre, 0), jnp.sum(cotangent.astype(jnp.float32), 0))


def quantize(rows):
    top = jnp.max(jnp.abs(rows), axis=1, keepdims=True)
    unit = jnp.maximum(top, 1e-30) * (1.0 / 32767.0)
    codes = jnp.round(rows * (1.0 / unit)).astype(jnp.int16)
    return codes, unit


def fold_coefs(gram):
    count = gram.shape[-1]
    width = count
    row_of = lax.broadcasted_iota(jnp.int32, (count, count), 0)
    col_of = lax.broadcasted_iota(jnp.int32, (count, count), 1)
    weight_row = jnp.ones((1, count), jnp.float32)
    inner = gram
    while width > 1:
        half = width // 2
        first = row_of % width < half
        own = (row_of == col_of).astype(jnp.float32)
        own_row = jnp.sum(inner * own, axis=0, keepdims=True)
        own_col = jnp.sum(inner * own, axis=1, keepdims=True)
        cross = (row_of % half == col_of % half) & (row_of != col_of)
        cross = (cross & (row_of < width) & (col_of < width)).astype(jnp.float32)
        cross_row = jnp.sum(inner * cross, axis=0, keepdims=True)
        cross_col = jnp.sum(inner * cross, axis=1, keepdims=True)
        coef_row = 1.0 - cross_row / (2.0 * (own_row + eps_norm))
        coef_col = 1.0 - cross_col / (2.0 * (own_col + eps_norm))
        scaled = jnp.where((row_of < width) & (col_of < width), inner * coef_row * coef_col, 0.0)
        leaf = (row_of == col_of % width).astype(jnp.float32)
        weight_row = weight_row * jnp.sum(leaf * coef_col, axis=0, keepdims=True)
        folded = scaled + pltpu.roll(scaled, count - half, 0)
        folded = folded + pltpu.roll(folded, count - half, 1)
        inner = jnp.where((row_of < half) & (col_of < half), folded, 0.0)
        width = half
    return weight_row


def coef_kernel(gram_ref, coef_ref):
    rows = [fold_coefs(gram_ref[now]) for now in range(4)]
    coef_ref[...] = jnp.concatenate(rows + [jnp.zeros((4, rows[0].shape[1]), jnp.float32)], axis=0)


def body(inputs, grads_out, lengths, w_in, bias_in, w_out):
    cotangent = masked_cotangent(grads_out, lengths)
    node_count = lax.axis_size("node")
    replicas = lax.axis_size("replica")
    width_model = inputs.shape[1]
    both = lax.all_gather(jnp.concatenate((inputs, cotangent), axis=1), "node", axis=0, tiled=True)
    terms = layer_grads(both[:, :width_model], both[:, width_model:], w_in, bias_in, w_out)
    share = width_model // node_count
    bias_share = lax.dynamic_slice_in_dim(terms[3], lax.axis_index("node") * share, share)
    codes_in, unit_in = quantize(terms[0])
    codes_out, unit_out = quantize(terms[1])
    codes = jnp.concatenate((codes_in.reshape(replicas, -1), codes_out.reshape(replicas, -1)), axis=1)
    small = jnp.concatenate(
        [v.reshape(replicas, -1) for v in (unit_in, unit_out, terms[2], bias_share)], axis=1
    )
    codes = lax.all_to_all(codes, "replica", 0, 0, tiled=True)
    small = lax.all_to_all(small, "replica", 0, 0, tiled=True)
    rows_in = terms[0].shape[0] // replicas
    rows_out = terms[1].shape[0] // replicas
    rows_bias = terms[2].shape[0] // replicas
    size_in = terms[0].size // replicas
    part_in = codes[:, :size_in].astype(jnp.float32).reshape(replicas, rows_in, -1) * small[:, :rows_in, None]
    part_out = (
        codes[:, size_in:].astype(jnp.float32).reshape(replicas, rows_out, -1)
        * small[:, rows_in : rows_in + rows_out, None]
    )
    rest = small[:, rows_in + rows_out :]
    parts = [part_in.reshape(replicas, -1), part_out.reshape(replicas, -1), rest[:, :rows_bias], rest[:, rows_bias:]]
    gram = jnp.stack(
        [
            lax.dot_general(
                p, p, (((1,), (1,)), ((), ())), precision=lax.Precision.HIGHEST, preferred_element_type=jnp.float32
            )
            for p in parts
        ]
    )
    gram = lax.psum(gram, ("node", "replica"))
    coefs = pl.pallas_call(
        coef_kernel, out_shape=jax.ShapeDtypeStruct((8, replicas), jnp.float32), name="tree_coefs"
    )(gram)
    outs = [jnp.sum(p * coefs[now][:, None], axis=0) for now, p in enumerate(parts)]
    return (outs[0].reshape(rows_in, -1), outs[1].reshape(rows_out, -1), outs[2], outs[3])


def solution(mesh):
    placed = (
        P(("node", "replica"), None),
        P(("node", "replica"), None),
        P(("node", "replica")),
        P(None, "node"),
        P("node"),
        P("node", None),
    )
    return jax.shard_map(
        body,
        mesh=mesh,
        in_specs=placed,
        out_specs=(
            P("replica", "node"),
            P(("node", "replica"), None),
            P(("node", "replica")),
            P(("node", "replica")),
        ),
        check_vma=False,
    )
```

```python
import functools

import jax
import jax.numpy as jnp
from jax import lax
from jax.experimental import pallas as pl
from jax.experimental.pallas import tpu as pltpu
from jax.sharding import PartitionSpec as P

SEQ = 128
MESH = pl.DeviceIdType.MESH
HALF = 256

root_half = 0.7071067811865476
inv_root_tau = 0.3989422804014327
eps_norm = 1e-06


def remote(src, dst, send_sem, recv_sem, device_id):
    return pltpu.make_async_remote_copy(
        src_ref=src, dst_ref=dst, send_sem=send_sem, recv_sem=recv_sem, device_id=device_id, device_id_type=MESH
    )


def grads_kernel(
    x_ref, g_ref, len_ref, w_in, bias_ref, w_out,
    code_in, code_out, small_ref,
    xb, cb, gin, gout, bsum, csum, small, send_sem, recv_sem, own_sem,
):
    me = lax.axis_index("node")
    count = lax.axis_size("node")
    right, left = {"node": (me + 1) % count}, {"node": (me + count - 1) % count}
    barrier = pltpu.get_barrier_semaphore()
    for neighbour in (left, right):
        pl.semaphore_signal(barrier, inc=1, device_id=neighbour, device_id_type=MESH)

    own = [pltpu.make_async_copy(x_ref.at[pl.ds(h * HALF, HALF)], xb.at[h], own_sem.at[h]) for h in range(2)]
    for copy in own:
        copy.start()
    for seq in range(g_ref.shape[0] // SEQ):
        rows = lax.broadcasted_iota(jnp.int32, (SEQ, g_ref.shape[1]), 0)
        part = g_ref[seq * SEQ : (seq + 1) * SEQ, :]
        at = seq * SEQ % HALF
        cb[seq * SEQ // HALF, at : at + SEQ, :] = jnp.where(rows < len_ref[seq], part, jnp.zeros_like(part))
    gin[...] = jnp.zeros_like(gin)
    gout[...] = jnp.zeros_like(gout)
    bsum[...] = jnp.zeros_like(bsum)
    csum[...] = jnp.zeros_like(csum)
    for copy in own:
        copy.wait()
    pl.semaphore_wait(barrier, 2)

    def pair(index, src, dst, target):
        return [remote(buf.at[src], buf.at[dst], send_sem.at[t, index], recv_sem.at[t, index], target)
                for t, buf in enumerate((xb, cb))]

    to_right = [pair(0, 0, 2, right), pair(1, 1, 3, right), pair(2, 2, 6, right)]
    to_left = [pair(3, 1, 5, left), pair(4, 0, 4, left), pair(5, 5, 7, left)]

    def start(copies):
        for copy in copies:
            copy.start()

    def arrived(copies):
        for copy in copies:
            copy.wait_recv()

    def compute(first, step):
        def one(now, carry):
            at = first + step * now
            x, c = xb[at], cb[at]
            preact = jnp.dot(x, w_in[...], preferred_element_type=jnp.float32) + bias_ref[...]
            normal_cdf = 0.5 * (1.0 + lax.erf(preact * root_half))
            activated = (preact * normal_cdf).astype(jnp.bfloat16)
            grad_act = lax.dot_general(c, w_out[...], (((1,), (1,)), ((), ())), preferred_element_type=jnp.float32)
            grad_pre = grad_act * (normal_cdf + preact * inv_root_tau * jnp.exp(-0.5 * preact * preact))
            grad_half = grad_pre.astype(jnp.bfloat16)
            gin[...] += lax.dot_general(x, grad_half, (((0,), (0,)), ((), ())), preferred_element_type=jnp.float32)
            gout[...] += lax.dot_general(activated, c, (((0,), (0,)), ((), ())), preferred_element_type=jnp.float32)
            bsum[...] += jnp.sum(grad_pre, axis=0, keepdims=True)
            csum[...] += jnp.sum(c.astype(jnp.float32), axis=0, keepdims=True)
            return carry

        lax.fori_loop(0, 2, one, 0)

    for a, b in zip(to_right[:2], to_left[:2]):
        start(a)
        start(b)
    compute(0, 1)
    arrived(to_right[0])
    start(to_right[2])
    arrived(to_left[0])
    start(to_left[2])
    compute(2, 3)
    arrived(to_right[1])
    arrived(to_left[1])
    compute(3, 1)
    arrived(to_right[2])
    arrived(to_left[2])
    compute(6, 1)
    for copies in to_right + to_left:
        for copy in copies:
            copy.wait_send()

    replicas = code_in.shape[0]
    group = 8
    rows_in, rows_out, rows_bias = code_in.shape[1], code_out.shape[1], bsum.shape[1] // replicas

    def codes(values, rows, first_lane):
        top = jnp.max(jnp.abs(values), axis=1, keepdims=True)
        unit = jnp.maximum(top, 1e-30) * (1.0 / 32767.0)
        code = jnp.round(values * (1.0 / unit)).astype(jnp.int16)
        lane = lax.broadcasted_iota(jnp.int32, (group * rows, 128), 1)
        row = lax.broadcasted_iota(jnp.int32, (group * rows, 128), 0)
        placed = jnp.where(lane - first_lane == row % rows, unit, 0.0)
        return code.reshape(group, rows, values.shape[1]), jnp.sum(placed.reshape(group, rows, 128), axis=1)

    def quantize(now, carry):
        block = pl.ds(pl.multiple_of(now * group, group), group)
        values = gin[pl.ds(pl.multiple_of(now * group * rows_in, group * rows_in), group * rows_in), :]
        code_in[block], unit_in = codes(values, rows_in, 0)
        values = gout[pl.ds(pl.multiple_of(now * group * rows_out, group * rows_out), group * rows_out), :]
        code_out[block], unit_out = codes(values, rows_out, rows_in)
        small[block, :] = unit_in + unit_out
        return carry

    lax.fori_loop(0, replicas // group, quantize, 0)

    def spread(values, per, first_lane):
        width = values.shape[1]
        row = lax.broadcasted_iota(jnp.int32, (replicas, width), 0)
        lane = lax.broadcasted_iota(jnp.int32, (replicas, width), 1)
        mine = jnp.where(lane // per == row, values, 0.0)
        source = lax.broadcasted_iota(jnp.int32, (width, 128), 0)
        target = lax.broadcasted_iota(jnp.int32, (width, 128), 1)
        pick = (target - first_lane == source % per).astype(jnp.float32)
        return jnp.dot(mine, pick, precision=lax.Precision.HIGHEST, preferred_element_type=jnp.float32)

    share = csum.shape[1] // 4
    mine = csum[:, pl.ds(pl.multiple_of(me * share, share), share)]
    total = small[...] + spread(bsum[...], rows_bias, rows_in + rows_out)
    total = total + spread(mine, share // replicas, rows_in + rows_out + rows_bias)
    small_ref[...] = total.reshape(replicas, 1, 128)


def gather_and_grads(inputs, grads_out, lengths, w_in, bias_in, w_out, replicas):
    rows, width = inputs.shape
    hidden = w_in.shape[1]
    vmem = pl.BlockSpec(memory_space=pltpu.VMEM)
    return pl.pallas_call(
        grads_kernel,
        out_shape=(
            jax.ShapeDtypeStruct((replicas, width // replicas, hidden), jnp.int16),
            jax.ShapeDtypeStruct((replicas, hidden // replicas, width), jnp.int16),
            jax.ShapeDtypeStruct((replicas, 1, 128), jnp.float32),
        ),
        in_specs=[pl.BlockSpec(memory_space=pl.ANY), vmem, pl.BlockSpec(memory_space=pltpu.SMEM), vmem, vmem, vmem],
        out_specs=(vmem, vmem, vmem),
        scratch_shapes=[
            pltpu.VMEM((8, HALF, width), jnp.bfloat16),
            pltpu.VMEM((8, HALF, width), jnp.bfloat16),
            pltpu.VMEM((width, hidden), jnp.float32),
            pltpu.VMEM((hidden, width), jnp.float32),
            pltpu.VMEM((1, hidden), jnp.float32),
            pltpu.VMEM((1, width), jnp.float32),
            pltpu.VMEM((replicas, 128), jnp.float32),
            pltpu.SemaphoreType.DMA((2, 6)),
            pltpu.SemaphoreType.DMA((2, 6)),
            pltpu.SemaphoreType.DMA((2,)),
        ],
        compiler_params=pltpu.CompilerParams(collective_id=0, has_side_effects=True),
        name="gather_grads",
    )(inputs, grads_out, lengths, w_in, bias_in, w_out)


def exchange_kernel(*refs):
    srcs, dsts = refs[:3], refs[3:6]
    send_sem, recv_sem, own_sem = refs[6:]
    me = lax.axis_index("replica")
    replicas = lax.axis_size("replica")
    core, y, z = me % 2, me // 2 % 4, me // 8
    barrier = pltpu.get_barrier_semaphore()

    def greet(step, carry):
        pl.semaphore_signal(barrier, inc=1, device_id={"replica": (me + step) % replicas}, device_id_type=MESH)
        return carry

    lax.fori_loop(1, replicas, greet, 0)
    own = [pltpu.make_async_copy(s.at[me], d.at[me], own_sem.at[t]) for t, (s, d) in enumerate(zip(srcs, dsts))]
    for copy in own:
        copy.start()
    pl.semaphore_wait(barrier, replicas - 1)

    def send(step, carry):
        place = step // 2
        other_z = (z + 3 * place) % 8
        other_y = (y + place + place // 8) % 4
        other = other_z * 8 + other_y * 2 + (core + step) % 2
        for t, (s, d) in enumerate(zip(srcs, dsts)):
            remote(s.at[other], d.at[me], send_sem.at[t], recv_sem.at[t], {"replica": other}).start()
        return carry

    lax.fori_loop(1, replicas, send, 0)
    for copy in own:
        copy.wait()
    for t, (s, d) in enumerate(zip(srcs, dsts)):
        others = pl.ds(0, replicas - 1)
        all_copies = remote(s.at[others], d.at[others], send_sem.at[t], recv_sem.at[t], {"replica": (me + 1) % replicas})
        all_copies.wait_send()
        all_copies.wait_recv()


def exchange(arrays):
    anywhere = pl.BlockSpec(memory_space=pl.ANY)
    return pl.pallas_call(
        exchange_kernel,
        out_shape=tuple(jax.ShapeDtypeStruct(a.shape, a.dtype) for a in arrays),
        in_specs=[anywhere] * 3,
        out_specs=(anywhere,) * 3,
        scratch_shapes=[
            pltpu.SemaphoreType.DMA((3,)),
            pltpu.SemaphoreType.DMA((3,)),
            pltpu.SemaphoreType.DMA((3,)),
        ],
        compiler_params=pltpu.CompilerParams(collective_id=1, has_side_effects=True),
        name="exchange",
    )(*arrays)


def fold_coefs(gram):
    count = gram.shape[-1]
    width = count
    row_of = lax.broadcasted_iota(jnp.int32, (count, count), 0)
    col_of = lax.broadcasted_iota(jnp.int32, (count, count), 1)
    weight = jnp.ones((count, 1), jnp.float32)
    inner = gram
    while width > 1:
        half = width // 2
        own = (row_of == col_of).astype(jnp.float32)
        own_row = jnp.sum(inner * own, axis=0, keepdims=True)
        own_col = jnp.sum(inner * own, axis=1, keepdims=True)
        cross = (row_of % half == col_of % half) & (row_of != col_of)
        cross = (cross & (row_of < width) & (col_of < width)).astype(jnp.float32)
        cross_row = jnp.sum(inner * cross, axis=0, keepdims=True)
        cross_col = jnp.sum(inner * cross, axis=1, keepdims=True)
        coef_row = 1.0 - cross_row / (2.0 * (own_row + eps_norm))
        coef_col = 1.0 - cross_col / (2.0 * (own_col + eps_norm))
        scaled = jnp.where((row_of < width) & (col_of < width), inner * coef_row * coef_col, 0.0)
        leaf = (row_of % width == col_of).astype(jnp.float32)
        weight = weight * jnp.sum(leaf * coef_row, axis=1, keepdims=True)
        folded = scaled + pltpu.roll(scaled, count - half, 0)
        folded = folded + pltpu.roll(folded, count - half, 1)
        inner = jnp.where((row_of < half) & (col_of < half), folded, 0.0)
        width = half
    return weight


def combine_kernel(
    code_in, code_out, small_ref,
    out_in, out_out, out_small,
    raw_in, raw_out, part_in, part_out, gram, core_slot, y_slot, x_slot, z_slot, last_slot, held, send_sem, recv_sem,
):
    replicas, rows_in, hidden = code_in.shape
    rows_out, width = code_out.shape[1:]
    me, node = lax.axis_index("replica"), lax.axis_index("node")
    core, y, z = me % 2, me // 2 % 4, me // 8
    partner = {"replica": me - core + (1 - core)}
    over_y = [{"replica": z * 8 + (y + k) % 4 * 2 + core} for k in range(1, 4)]
    over_x = [{"node": (node + k) % 4} for k in range(1, 4)]
    over_z = [{"replica": (z + k) % 8 * 8 + y * 2 + core} for k in range(1, 8)]
    barrier = pltpu.get_barrier_semaphore()
    peers = [partner] + over_y + over_x + over_z
    for peer in peers:
        pl.semaphore_signal(barrier, inc=1, device_id=peer, device_id_type=MESH)

    def widen(now, carry):
        raw_in[now] = code_in[now].astype(jnp.float32)
        raw_out[now] = code_out[now].astype(jnp.float32)
        return carry

    lax.fori_loop(0, replicas, widen, 0)
    small = small_ref[...].reshape(replicas, 128)
    for row in range(rows_in):
        part_in[:, row * hidden : (row + 1) * hidden] = raw_in[:, row, :] * small[:, row : row + 1]
    for row in range(rows_out):
        part_out[:, row * width : (row + 1) * width] = raw_out[:, row, :] * small[:, rows_in + row : rows_in + row + 1]

    def products(part):
        return lax.dot_general(
            part, part, (((1,), (1,)), ((), ())), precision=lax.Precision.HIGHEST, preferred_element_type=jnp.float32
        )

    lane = lax.broadcasted_iota(jnp.int32, (replicas, 128), 1)
    first_bias = rows_in + rows_out
    rows_bias, rows_last = hidden // replicas, width // 4 // replicas
    bias_in = jnp.where((lane >= first_bias) & (lane < first_bias + rows_bias), small, 0.0)
    bias_out = jnp.where((lane >= first_bias + rows_bias) & (lane < first_bias + rows_bias + rows_last), small, 0.0)
    gram[0] = jnp.concatenate([products(part_in[...]), products(part_out[...])], axis=1)
    gram[1] = jnp.concatenate([products(bias_in), products(bias_out)], axis=1)
    pl.semaphore_wait(barrier, len(peers))

    def stage(first, source, slots, targets):
        copies = [
            remote(source, slots.at[k], send_sem.at[first + k], recv_sem.at[first + k], target)
            for k, target in enumerate(targets)
        ]
        for copy in copies:
            copy.start()
        for copy in copies:
            copy.wait()

    stage(0, gram.at[1 - core], core_slot, [partner])
    held[0] = gram[core] + core_slot[0]
    stage(1, held.at[0], y_slot, over_y)
    held[1] = held[0] + (y_slot[0] + y_slot[1] + y_slot[2])
    stage(4, held.at[1], x_slot, over_x)
    held[2] = held[1] + (x_slot[0] + x_slot[1] + x_slot[2])
    stage(7, held.at[2], z_slot, over_z)
    total = held[2]
    for k in range(7):
        total = total + z_slot[k]
    held[3] = total
    stage(14, held.at[3], last_slot, [partner])
    other = last_slot[0]
    is_first = core == 0
    main = jnp.where(is_first, total, other)
    rest = jnp.where(is_first, other, total)

    weights = [fold_coefs(g[:, s : s + replicas]) for g in (main, rest) for s in (0, replicas)]
    for row in range(rows_in):
        part = part_in[:, row * hidden : (row + 1) * hidden]
        out_in[row : row + 1, :] = jnp.sum(part * weights[0], axis=0, keepdims=True)
    for row in range(rows_out):
        part = part_out[:, row * width : (row + 1) * width]
        out_out[row : row + 1, :] = jnp.sum(part * weights[1], axis=0, keepdims=True)
    bias = bias_in * weights[2] + bias_out * weights[3]
    out_small[...] = jnp.broadcast_to(jnp.sum(bias, axis=0, keepdims=True), out_small.shape)


def combine(arrays):
    replicas, rows_in, hidden = arrays[0].shape
    rows_out, width = arrays[1].shape[1:]
    vmem = pl.BlockSpec(memory_space=pltpu.VMEM)
    return pl.pallas_call(
        combine_kernel,
        out_shape=(
            jax.ShapeDtypeStruct((rows_in, hidden), jnp.float32),
            jax.ShapeDtypeStruct((rows_out, width), jnp.float32),
            jax.ShapeDtypeStruct((8, 128), jnp.float32),
        ),
        in_specs=[vmem] * 3,
        out_specs=(vmem,) * 3,
        scratch_shapes=[
            pltpu.VMEM(arrays[0].shape, jnp.float32),
            pltpu.VMEM(arrays[1].shape, jnp.float32),
            pltpu.VMEM((replicas, rows_in * hidden), jnp.float32),
            pltpu.VMEM((replicas, rows_out * width), jnp.float32),
            pltpu.VMEM((2, replicas, 128), jnp.float32),
            pltpu.VMEM((1, replicas, 128), jnp.float32),
            pltpu.VMEM((3, replicas, 128), jnp.float32),
            pltpu.VMEM((3, replicas, 128), jnp.float32),
            pltpu.VMEM((7, replicas, 128), jnp.float32),
            pltpu.VMEM((1, replicas, 128), jnp.float32),
            pltpu.VMEM((4, replicas, 128), jnp.float32),
            pltpu.SemaphoreType.DMA((15,)),
            pltpu.SemaphoreType.DMA((15,)),
        ],
        compiler_params=pltpu.CompilerParams(collective_id=2, has_side_effects=True),
        name="combine",
    )(*arrays)


def body(inputs, grads_out, lengths, w_in, bias_in, w_out):
    replicas = lax.axis_size("replica")
    bias_row = bias_in.astype(jnp.float32).reshape(1, -1)
    arrays = gather_and_grads(inputs, grads_out, lengths, w_in, bias_row, w_out, replicas)
    arrays = exchange(arrays)
    out_in, out_out, out_small = combine(arrays)
    rows_in, rows_out = out_in.shape[0], out_out.shape[0]
    first = rows_in + rows_out
    middle = first + w_in.shape[1] // replicas
    last = middle + inputs.shape[1] // 4 // replicas
    return (out_in, out_out, out_small[0, first:middle], out_small[0, middle:last])


def solution(mesh):
    placed = (
        P(("node", "replica"), None),
        P(("node", "replica"), None),
        P(("node", "replica")),
        P(None, "node"),
        P("node"),
        P("node", None),
    )
    return jax.shard_map(
        body,
        mesh=mesh,
        in_specs=placed,
        out_specs=(
            P("replica", "node"),
            P(("node", "replica"), None),
            P(("node", "replica")),
            P(("node", "replica")),
        ),
        check_vma=False,
    )
```

```python
import jax
import jax.numpy as jnp
from jax import lax
from jax.experimental import pallas as pl
from jax.experimental.pallas import tpu as pltpu
from jax.sharding import PartitionSpec as P

SEQ = 128
MESH = pl.DeviceIdType.MESH
HALF = 256

root_half = 0.7071067811865476
inv_root_tau = 0.3989422804014327
eps_norm = 1e-06


def remote(src, dst, send_sem, recv_sem, device_id):
    return pltpu.make_async_remote_copy(
        src_ref=src, dst_ref=dst, send_sem=send_sem, recv_sem=recv_sem, device_id=device_id, device_id_type=MESH
    )


def grads_kernel(
    x_ref, g_ref, len_ref, w_in, bias_ref, w_out,
    all_in, all_out, all_small,
    xb, cb, gb, wi, wo, gin, gout, bsum, csum, small, code_in, code_out, small_msg,
    load_sem, send_sem, recv_sem, relay_send, relay_recv, out_send, in_recv, rows_recv, small_recv, own_sem,
):
    node, nodes = lax.axis_index("node"), lax.axis_size("node")
    me, replicas = lax.axis_index("replica"), lax.axis_size("replica")
    core, y, z = me % 2, me // 2 % 4, me // 8
    hidden = wi.shape[1]
    right, left = {"node": (node + 1) % nodes}, {"node": (node + nodes - 1) % nodes}
    partner = {"replica": me - core + (1 - core)}
    barrier = pltpu.get_barrier_semaphore()
    for neighbour in (left, right):
        pl.semaphore_signal(barrier, inc=1, device_id=neighbour, device_id_type=MESH)

    def greet(step, carry):
        pl.semaphore_signal(barrier, inc=1, device_id={"replica": (me + step) % replicas}, device_id_type=MESH)
        return carry

    lax.fori_loop(1, replicas, greet, 0)

    columns = pl.ds(pl.multiple_of(core * hidden, hidden), hidden)
    loads = [
        pltpu.make_async_copy(g_ref, gb, load_sem.at[0]),
        pltpu.make_async_copy(x_ref.at[pl.ds(0, HALF)], xb.at[core * 8], load_sem.at[1]),
        pltpu.make_async_copy(x_ref.at[pl.ds(HALF, HALF)], xb.at[core * 8 + 1], load_sem.at[2]),
        pltpu.make_async_copy(w_in.at[:, columns], wi, load_sem.at[3]),
        pltpu.make_async_copy(w_out.at[columns], wo, load_sem.at[4]),
    ]
    for copy in loads:
        copy.start()
    loads[0].wait()
    for seq in range(g_ref.shape[0] // SEQ):
        rows = lax.broadcasted_iota(jnp.int32, (SEQ, g_ref.shape[1]), 0)
        part = gb[seq * SEQ : (seq + 1) * SEQ, :]
        at = seq * SEQ % HALF
        cb[core * 8 + seq * SEQ // HALF, at : at + SEQ, :] = jnp.where(rows < len_ref[seq], part, jnp.zeros_like(part))
    for copy in loads[1:]:
        copy.wait()
    pl.semaphore_wait(barrier, replicas + 1)

    def pair(index, src, dst, target):
        return [remote(buf.at[core * 8 + src], buf.at[core * 8 + dst], send_sem.at[t, index], recv_sem.at[t, index], target)
                for t, buf in enumerate((xb, cb))]

    to_right = [pair(0, 0, 2, right), pair(1, 1, 3, right), pair(2, 2, 6, right)]
    to_left = [pair(3, 1, 5, left), pair(4, 0, 4, left), pair(5, 5, 7, left)]

    def relay(owner, chunk):
        return [remote(buf.at[owner * 8 + chunk], buf.at[owner * 8 + chunk], relay_send.at[t, chunk],
                       relay_recv.at[t, chunk], partner) for t, buf in enumerate((xb, cb))]

    def start(copies):
        for copy in copies:
            copy.start()

    def arrived(copies):
        for copy in copies:
            copy.wait_recv()

    def left_here(copies):
        for copy in copies:
            copy.wait_send()

    def send_own():
        for a, b in zip(to_right[:2], to_left[:2]):
            start(a)
            start(b)

    @pl.when(core == 0)
    def _():
        send_own()

    start(relay(core, 0))
    start(relay(core, 1))

    rows_in, rows_out = code_in.shape[2], code_out.shape[2]
    rows_bias = rows_out
    group = 8
    bias = bias_ref[:, columns]

    def codes(values, count, rows, first_lane):
        top = jnp.max(jnp.abs(values), axis=1, keepdims=True)
        unit = jnp.maximum(top, 1e-30) * (1.0 / 32767.0)
        code = jnp.round(values * (1.0 / unit)).astype(jnp.int16)
        lane = lax.broadcasted_iota(jnp.int32, (count * rows, 128), 1)
        row = lax.broadcasted_iota(jnp.int32, (count * rows, 128), 0)
        placed = jnp.where(lane - first_lane == row % rows, unit, 0.0)
        return code.reshape(count, rows, values.shape[1]), jnp.sum(placed.reshape(count, rows, 128), axis=1)

    def spread(values, targets, per, first_lane):
        width = values.shape[1]
        row = lax.broadcasted_iota(jnp.int32, (targets, width), 0)
        lane = lax.broadcasted_iota(jnp.int32, (targets, width), 1)
        mine = jnp.where(lane // per == row, values, 0.0)
        source = lax.broadcasted_iota(jnp.int32, (width, 128), 0)
        target = lax.broadcasted_iota(jnp.int32, (width, 128), 1)
        pick = (target - first_lane == source % per).astype(jnp.float32)
        return jnp.dot(mine, pick, precision=lax.Precision.HIGHEST, preferred_element_type=jnp.float32)

    def one_replica(owner, carry):
        mine = core == owner

        def compute(chunks):
            first, step, count = chunks

            def one(now, carry):
                at = owner * 8 + first + step * now
                x, c = xb[at], cb[at]
                preact = jnp.dot(x, wi[...], preferred_element_type=jnp.float32) + bias
                normal_cdf = 0.5 * (1.0 + lax.erf(preact * root_half))
                activated = (preact * normal_cdf).astype(jnp.bfloat16)
                grad_act = lax.dot_general(c, wo[...], (((1,), (1,)), ((), ())), preferred_element_type=jnp.float32)
                grad_pre = grad_act * (normal_cdf + preact * inv_root_tau * jnp.exp(-0.5 * preact * preact))
                grad_half = grad_pre.astype(jnp.bfloat16)
                gout[...] += lax.dot_general(activated, c, (((0,), (0,)), ((), ())), preferred_element_type=jnp.float32)
                gin[...] += lax.dot_general(grad_half, x, (((0,), (0,)), ((), ())), preferred_element_type=jnp.float32)
                bsum[...] += jnp.sum(grad_pre, axis=0, keepdims=True)
                csum[...] += jnp.sum(c.astype(jnp.float32), axis=0, keepdims=True)
                return carry

            lax.fori_loop(0, count, one, 0)

        def receive(ring, chunks, forwards=()):
            @pl.when(mine)
            def _():
                for copies, chunk in zip(ring, chunks):
                    arrived(copies)
                for copies in forwards:
                    start(copies)
                for chunk in chunks:
                    start(relay(owner, chunk))

            @pl.when(jnp.logical_not(mine))
            def _():
                for chunk in chunks:
                    arrived(relay(owner, chunk))

        gin[...] = jnp.zeros_like(gin)
        gout[...] = jnp.zeros_like(gout)
        bsum[...] = jnp.zeros_like(bsum)
        csum[...] = jnp.zeros_like(csum)

        @pl.when(jnp.logical_not(mine))
        def _():
            arrived(relay(owner, 0))
            arrived(relay(owner, 1))

        receive((to_right[0], to_left[0]), (2, 5), (to_right[2], to_left[2]))
        compute((0, 1, 2))
        compute((2, 3, 2))
        receive((to_right[1], to_left[1]), (3, 4))

        @pl.when(jnp.logical_and(owner == 0, core == 1))
        def _():
            send_own()

        compute((3, 1, 2))
        receive((to_right[2], to_left[2]), (6, 7))
        compute((6, 1, 2))

        def quantize(now, carry):
            width = group * rows_in
            values = gin[:, pl.ds(pl.multiple_of(now * width, width), width)].T
            block = pl.ds(pl.multiple_of(now * group, group), group)
            code_in[owner, block], small[block, :] = codes(values, group, rows_in, 0)
            return carry

        lax.fori_loop(0, replicas // group, quantize, 0)
        half = replicas // 2

        def quantize_out(now, carry):
            height = group * rows_out
            values = gout[pl.ds(pl.multiple_of(now * height, height), height), :]
            code_out[owner, pl.ds(pl.multiple_of(now * group, group), group)], unit = codes(values, group, rows_out, rows_in)
            at = pl.multiple_of(core * half + now * group, group)
            small[pl.ds(at, group), :] += unit
            return carry

        lax.fori_loop(0, half // group, quantize_out, 0)
        kept = pl.ds(pl.multiple_of(core * half, half), half)
        small[kept, :] += spread(bsum[...], half, rows_bias, rows_in + rows_out)
        share = csum.shape[1] // 4
        mine_now = csum[:, pl.ds(pl.multiple_of(node * share, share), share)]
        total = small[...] + spread(mine_now, replicas, share // replicas, rows_in + rows_out + rows_bias)
        small_msg[owner] = total.reshape(replicas, 1, 128)

        source = me - core + owner
        pltpu.make_async_copy(code_in.at[owner, me], all_in.at[core, source], own_sem.at[owner, 0]).start()
        pltpu.make_async_copy(small_msg.at[owner, me], all_small.at[core, source], own_sem.at[owner, 1]).start()

        @pl.when(me // half == core)
        def _():
            pltpu.make_async_copy(code_out.at[owner, me % half], all_out.at[source], own_sem.at[owner, 2]).start()

        def send(step, carry):
            place = step // 2
            other_z = (z + 3 * place) % 8
            other_y = (y + place + place // 8) % 4
            other = other_z * 8 + other_y * 2 + (core + step) % 2
            target = {"replica": other}
            remote(code_in.at[owner, other], all_in.at[core, source], out_send.at[owner, 0], in_recv.at[core], target).start()
            remote(
                small_msg.at[owner, other], all_small.at[core, source], out_send.at[owner, 1], small_recv.at[core], target
            ).start()

            @pl.when(other // half == core)
            def _():
                remote(
                    code_out.at[owner, other % half], all_out.at[source], out_send.at[owner, 2], rows_recv, target
                ).start()

            return carry

        lax.fori_loop(1, replicas, send, 0)
        return carry

    lax.fori_loop(0, 2, one_replica, 0)

    for copies in to_right + to_left:
        left_here(copies)
    for chunk in range(8):
        left_here(relay(core, chunk))
    half = replicas // 2
    keeps = me // half == core
    others = pl.ds(0, replicas - 1)
    for owner in range(2):
        pltpu.make_async_copy(code_in.at[owner, me], all_in.at[core, me], own_sem.at[owner, 0]).wait()
        pltpu.make_async_copy(small_msg.at[owner, me], all_small.at[core, me], own_sem.at[owner, 1]).wait()
        remote(code_in.at[owner, others], all_in.at[core, others], out_send.at[owner, 0], in_recv.at[core], partner).wait_send()
        remote(
            small_msg.at[owner, others], all_small.at[core, others], out_send.at[owner, 1], small_recv.at[core], partner
        ).wait_send()

        @pl.when(keeps)
        def _():
            some = pl.ds(0, half - 1)
            pltpu.make_async_copy(code_out.at[owner, me % half], all_out.at[me], own_sem.at[owner, 2]).wait()
            remote(code_out.at[owner, some], all_out.at[some], out_send.at[owner, 2], rows_recv, partner).wait_send()

        @pl.when(jnp.logical_not(keeps))
        def _():
            every = pl.ds(0, half)
            remote(code_out.at[owner, every], all_out.at[every], out_send.at[owner, 2], rows_recv, partner).wait_send()

    most = pl.ds(0, replicas - 2)
    remote(all_in.at[core, most], all_in.at[core, most], out_send.at[0, 0], in_recv.at[core], partner).wait_recv()
    remote(all_in.at[1 - core], all_in.at[1 - core], out_send.at[0, 0], in_recv.at[1 - core], partner).wait_recv()
    remote(all_small.at[core, most], all_small.at[core, most], out_send.at[0, 1], small_recv.at[core], partner).wait_recv()
    remote(all_small.at[1 - core], all_small.at[1 - core], out_send.at[0, 1], small_recv.at[1 - core], partner).wait_recv()

    @pl.when(keeps)
    def _():
        remote(all_out.at[most], all_out.at[most], out_send.at[0, 2], rows_recv, partner).wait_recv()

    @pl.when(jnp.logical_not(keeps))
    def _():
        remote(all_out, all_out, out_send.at[0, 2], rows_recv, partner).wait_recv()


def gather_and_grads(inputs, grads_out, lengths, w_in, bias_in, w_out, replicas):
    rows, width = inputs.shape
    hidden = w_in.shape[1] // 2
    rows_in, rows_out = width // replicas, 2 * hidden // replicas
    vmem = pl.BlockSpec(memory_space=pltpu.VMEM)
    anywhere = pl.BlockSpec(memory_space=pl.ANY)
    return pl.pallas_call(
        grads_kernel,
        out_shape=(
            jax.ShapeDtypeStruct((2, replicas, rows_in, hidden), jnp.int16),
            jax.ShapeDtypeStruct((replicas, rows_out, width), jnp.int16),
            jax.ShapeDtypeStruct((2, replicas, 1, 128), jnp.float32),
        ),
        in_specs=[anywhere, anywhere, pl.BlockSpec(memory_space=pltpu.SMEM), anywhere, vmem, anywhere],
        out_specs=(anywhere, anywhere, anywhere),
        scratch_shapes=[
            pltpu.VMEM((16, HALF, width), jnp.bfloat16),
            pltpu.VMEM((16, HALF, width), jnp.bfloat16),
            pltpu.VMEM((rows, width), jnp.bfloat16),
            pltpu.VMEM((width, hidden), jnp.bfloat16),
            pltpu.VMEM((hidden, width), jnp.bfloat16),
            pltpu.VMEM((hidden, width), jnp.float32),
            pltpu.VMEM((hidden, width), jnp.float32),
            pltpu.VMEM((1, hidden), jnp.float32),
            pltpu.VMEM((1, width), jnp.float32),
            pltpu.VMEM((replicas, 128), jnp.float32),
            pltpu.VMEM((2, replicas, rows_in, hidden), jnp.int16),
            pltpu.VMEM((2, replicas // 2, rows_out, width), jnp.int16),
            pltpu.VMEM((2, replicas, 1, 128), jnp.float32),
            pltpu.SemaphoreType.DMA((5,)),
            pltpu.SemaphoreType.DMA((2, 6)),
            pltpu.SemaphoreType.DMA((2, 6)),
            pltpu.SemaphoreType.DMA((2, 8)),
            pltpu.SemaphoreType.DMA((2, 8)),
            pltpu.SemaphoreType.DMA((2, 3)),
            pltpu.SemaphoreType.DMA((2,)),
            pltpu.SemaphoreType.DMA,
            pltpu.SemaphoreType.DMA((2,)),
            pltpu.SemaphoreType.DMA((2, 3)),
        ],
        compiler_params=pltpu.CompilerParams(collective_id=0, has_side_effects=True),
        name="gather_grads",
    )(inputs, grads_out, lengths, w_in, bias_in, w_out)


def fold_coefs(gram):
    count = gram.shape[-1]
    width = count
    row_of = lax.broadcasted_iota(jnp.int32, (count, count), 0)
    col_of = lax.broadcasted_iota(jnp.int32, (count, count), 1)
    weight = jnp.ones((count, 1), jnp.float32)
    inner = gram
    while width > 1:
        half = width // 2
        own = (row_of == col_of).astype(jnp.float32)
        own_row = jnp.sum(inner * own, axis=0, keepdims=True)
        own_col = jnp.sum(inner * own, axis=1, keepdims=True)
        cross = (row_of % half == col_of % half) & (row_of != col_of)
        cross = (cross & (row_of < width) & (col_of < width)).astype(jnp.float32)
        cross_row = jnp.sum(inner * cross, axis=0, keepdims=True)
        cross_col = jnp.sum(inner * cross, axis=1, keepdims=True)
        coef_row = 1.0 - cross_row / (2.0 * (own_row + eps_norm))
        coef_col = 1.0 - cross_col / (2.0 * (own_col + eps_norm))
        scaled = jnp.where((row_of < width) & (col_of < width), inner * coef_row * coef_col, 0.0)
        leaf = (row_of % width == col_of).astype(jnp.float32)
        weight = weight * jnp.sum(leaf * coef_row, axis=1, keepdims=True)
        folded = scaled + pltpu.roll(scaled, count - half, 0)
        folded = folded + pltpu.roll(folded, count - half, 1)
        inner = jnp.where((row_of < half) & (col_of < half), folded, 0.0)
        width = half
    return weight


def combine_kernel(
    code_in, code_out, small_ref,
    out_in, out_out, out_small,
    raw_in, raw_out, part_in, part_out, gram, core_slot, y_slot, x_slot, z_slot, last_slot, held, send_sem, recv_sem,
):
    replicas, rows_in, hidden = raw_in.shape
    rows_out, width = code_out.shape[1:]
    me, node = lax.axis_index("replica"), lax.axis_index("node")
    core, y, z = me % 2, me // 2 % 4, me // 8
    partner = {"replica": me - core + (1 - core)}
    over_y = [{"replica": z * 8 + (y + k) % 4 * 2 + core} for k in range(1, 4)]
    over_x = [{"node": (node + k) % 4} for k in range(1, 4)]
    over_z = [{"replica": (z + k) % 8 * 8 + y * 2 + core} for k in range(1, 8)]
    barrier = pltpu.get_barrier_semaphore()
    peers = [partner] + over_y + over_x + over_z
    for peer in peers:
        pl.semaphore_signal(barrier, inc=1, device_id=peer, device_id_type=MESH)

    def widen(now, carry):
        raw_in[now, :, : hidden // 2] = code_in[0, now].astype(jnp.float32)
        raw_in[now, :, hidden // 2 :] = code_in[1, now].astype(jnp.float32)
        raw_out[now] = code_out[now].astype(jnp.float32)
        return carry

    lax.fori_loop(0, replicas, widen, 0)
    halves = [small_ref[half].reshape(replicas, 128) for half in range(2)]
    small = jnp.where(me >= replicas // 2, halves[1], halves[0])
    for row in range(rows_in):
        for half in range(2):
            first, last = half * hidden // 2, (half + 1) * hidden // 2
            part = raw_in[:, row, first:last] * halves[half][:, row : row + 1]
            part_in[:, row * hidden + first : row * hidden + last] = part
    for row in range(rows_out):
        part_out[:, row * width : (row + 1) * width] = raw_out[:, row, :] * small[:, rows_in + row : rows_in + row + 1]

    def products(part):
        return lax.dot_general(
            part, part, (((1,), (1,)), ((), ())), precision=lax.Precision.HIGHEST, preferred_element_type=jnp.float32
        )

    lane = lax.broadcasted_iota(jnp.int32, (replicas, 128), 1)
    first_bias = rows_in + rows_out
    rows_bias, rows_last = hidden // replicas, width // 4 // replicas
    bias_in = jnp.where((lane >= first_bias) & (lane < first_bias + rows_bias), small, 0.0)
    bias_out = jnp.where((lane >= first_bias + rows_bias) & (lane < first_bias + rows_bias + rows_last), small, 0.0)
    gram[0] = jnp.concatenate([products(part_in[...]), products(part_out[...])], axis=1)
    gram[1] = jnp.concatenate([products(bias_in), products(bias_out)], axis=1)
    pl.semaphore_wait(barrier, len(peers))

    def stage(first, source, slots, targets):
        copies = [
            remote(source, slots.at[k], send_sem.at[first + k], recv_sem.at[first + k], target)
            for k, target in enumerate(targets)
        ]
        for copy in copies:
            copy.start()
        for copy in copies:
            copy.wait()

    stage(0, gram.at[1 - core], core_slot, [partner])
    held[0] = gram[core] + core_slot[0]
    stage(1, held.at[0], y_slot, over_y)
    held[1] = held[0] + (y_slot[0] + y_slot[1] + y_slot[2])
    stage(4, held.at[1], x_slot, over_x)
    held[2] = held[1] + (x_slot[0] + x_slot[1] + x_slot[2])
    stage(7, held.at[2], z_slot, over_z)
    total = held[2]
    for k in range(7):
        total = total + z_slot[k]
    held[3] = total
    stage(14, held.at[3], last_slot, [partner])
    other = last_slot[0]
    is_first = core == 0
    main = jnp.where(is_first, total, other)
    rest = jnp.where(is_first, other, total)

    weights = [fold_coefs(g[:, s : s + replicas]) for g in (main, rest) for s in (0, replicas)]
    for row in range(rows_in):
        part = part_in[:, row * hidden : (row + 1) * hidden]
        out_in[row : row + 1, :] = jnp.sum(part * weights[0], axis=0, keepdims=True)
    for row in range(rows_out):
        part = part_out[:, row * width : (row + 1) * width]
        out_out[row : row + 1, :] = jnp.sum(part * weights[1], axis=0, keepdims=True)
    bias = bias_in * weights[2] + bias_out * weights[3]
    out_small[...] = jnp.broadcast_to(jnp.sum(bias, axis=0, keepdims=True), out_small.shape)


def combine(arrays):
    halves, replicas, rows_in, hidden = arrays[0].shape
    hidden = halves * hidden
    rows_out, width = arrays[1].shape[1:]
    vmem = pl.BlockSpec(memory_space=pltpu.VMEM)
    return pl.pallas_call(
        combine_kernel,
        out_shape=(
            jax.ShapeDtypeStruct((rows_in, hidden), jnp.float32),
            jax.ShapeDtypeStruct((rows_out, width), jnp.float32),
            jax.ShapeDtypeStruct((8, 128), jnp.float32),
        ),
        in_specs=[vmem] * 3,
        out_specs=(vmem,) * 3,
        scratch_shapes=[
            pltpu.VMEM((replicas, rows_in, hidden), jnp.float32),
            pltpu.VMEM(arrays[1].shape, jnp.float32),
            pltpu.VMEM((replicas, rows_in * hidden), jnp.float32),
            pltpu.VMEM((replicas, rows_out * width), jnp.float32),
            pltpu.VMEM((2, replicas, 128), jnp.float32),
            pltpu.VMEM((1, replicas, 128), jnp.float32),
            pltpu.VMEM((3, replicas, 128), jnp.float32),
            pltpu.VMEM((3, replicas, 128), jnp.float32),
            pltpu.VMEM((7, replicas, 128), jnp.float32),
            pltpu.VMEM((1, replicas, 128), jnp.float32),
            pltpu.VMEM((4, replicas, 128), jnp.float32),
            pltpu.SemaphoreType.DMA((15,)),
            pltpu.SemaphoreType.DMA((15,)),
        ],
        compiler_params=pltpu.CompilerParams(collective_id=2, has_side_effects=True),
        name="combine",
    )(*arrays)


def body(inputs, grads_out, lengths, w_in, bias_in, w_out):
    replicas = lax.axis_size("replica")
    bias_row = bias_in.astype(jnp.float32).reshape(1, -1)
    arrays = gather_and_grads(inputs, grads_out, lengths, w_in, bias_row, w_out, replicas)
    out_in, out_out, out_small = combine(arrays)
    rows_in, rows_out = out_in.shape[0], out_out.shape[0]
    first = rows_in + rows_out
    middle = first + w_in.shape[1] // replicas
    last = middle + inputs.shape[1] // 4 // replicas
    return (out_in, out_out, out_small[0, first:middle], out_small[0, middle:last])


def solution(mesh):
    placed = (
        P(("node", "replica"), None),
        P(("node", "replica"), None),
        P(("node", "replica")),
        P(None, "node"),
        P("node"),
        P("node", None),
    )
    return jax.shard_map(
        body,
        mesh=mesh,
        in_specs=placed,
        out_specs=(
            P("replica", "node"),
            P(("node", "replica"), None),
            P(("node", "replica")),
            P(("node", "replica")),
        ),
        check_vma=False,
    )
```
